32 devices in a mesh: groups: 2 (over y), ctx: 4 (over z), tm: 2 (over x), tp: 2 (over core).
Axes of the slice: x: 2, y: 2, z: 4, core: 2. Of those that a mesh axis runs over, the one named last changes fastest.
Arguments:
- tokens: bfloat16 [256, 8, 1024], P(('groups', 'tm'), 'ctx'), parts along dimension 0, may hold values from -6 to 6
- norm_gain: float32 [1024], replicated, may hold values from 0.1 to 1.9
- block_mask: int32 [4, 4, 4], P(('groups', 'tm'), 'ctx'), parts along dimension 0, may hold values from 0 to 1, as said below
- w_query: bfloat16 [1024, 1024], P('tm', 'tp'), may hold values from -1.25 to 1.25
- w_key: bfloat16 [1024, 1024], P('tm', 'tp'), may hold values from -1.25 to 1.25
- w_value: bfloat16 [1024, 1024], P('tm', 'tp'), may hold values from -0.1875 to 0.1875
- w_out: bfloat16 [1024, 1024], P('tp', 'tm'), may hold values from -0.1875 to 0.1875
- w_up: bfloat16 [1024, 2048], P('tm', 'tp'), may hold values from -0.1875 to 0.1875
- w_down: bfloat16 [2048, 1024], P('tp', 'tm'), may hold values from -0.125 to 0.125
- conv_weight: float32 [5, 1024], P(None, 'tp'), may hold values from -2.5 to 2.5
Outputs:
- denoised: bfloat16 [256, 8, 1024], P(('groups', 'tm'), 'ctx', 'tp'), parts along dimension 0
The draws below stay inside these ranges and needn't reach their ends.
There are 2 independent parts, one for each index of `groups`. The reference program is written for one: setup_inputs(seed, part) draws one part's arguments, and reference() takes and returns one part's arrays. A program takes and returns all parts, laid end to end along the dimension named above; an argument that names none is the same for every part. Nothing has to cross between parts.
Inputs may be any that keep to these rules, and one draw needn't show every extreme that they name: block_mask[w, i, i] is 1 for every window w and block i.
All inputs are finite; a program needn't handle non-finite values.
Results may differ from the reference program's by a relative error of at most 0.0076.
Values may be sent and summed in bfloat16 or wider, within the bound.
A program may use at most 64 MiB of HBM per device.

```python
import jax
import jax.numpy as jnp
from jax import lax

D = 1024
HEADS = 16
HEAD_DIM = 64
FF = 2048
KERNEL = 5
DAN_DEV = 2
FRAME_DEV = 64
DANCERS = 8
FRAMES = 128
N_CTX = 4
N_TM = 2


def draw_block_mask(key, part):
    first = jax.random.fold_in(key, 11)
    second = jax.random.fold_in(key, 23)
    levels = jax.random.randint(first, (N_TM, N_CTX, 1), 1, 10)
    rolls = jax.random.randint(second, (N_TM, N_CTX, N_CTX), 0, 10)
    allowed = (rolls < levels).astype(jnp.int32)
    diagonal = jnp.eye(N_CTX, dtype=jnp.int32)[None, :, :]
    return jnp.maximum(allowed, diagonal)


def draw_tokens(key, part):
    noise = jax.random.normal(jax.random.fold_in(key, 7), (FRAMES, DANCERS, D), jnp.float32)
    return jnp.clip(noise, -6.0, 6.0).astype(jnp.bfloat16)


def drawn_weight(key, salt):
    scale = D ** (-0.5)
    drawn = jax.random.normal(jax.random.fold_in(key, salt), (D, D), jnp.float32)
    return jnp.clip(drawn * scale, -6.0 * scale, 6.0 * scale)


def draw_w_query(key, part):
    return drawn_weight(key, 201).astype(jnp.bfloat16)


def draw_w_key(key, part):
    return drawn_weight(key, 202).astype(jnp.bfloat16)


def level_of(key, dims, cuts, low, largest):
    def one(position, blocks):
        steps = jax.random.uniform(jax.random.fold_in(jax.random.fold_in(key, 6), position), (blocks,), jnp.float32, low / len(cuts), largest / len(cuts))
        return jnp.repeat(jnp.exp(steps), dims[position] // blocks).reshape((-1,) + (1,) * (len(dims) - position - 1))

    level = one(*cuts[0])
    for cut in cuts[1:]:
        level = level * one(*cut)
    return level


def scatter_about(own_key, shape, spread, reach, split=(), held_as=jnp.bfloat16):
    values = jax.random.normal(own_key, shape, jnp.float32) * spread
    if len(split) > 0:
        values = level_of(own_key, shape, split, -0.22, 0.18) * values
    return jnp.clip(values, min=-reach, max=reach).astype(held_as)


def setup_inputs(seed: int = 0, part: int = 0) -> dict:
    key_of = jax.random.split(jax.random.key(seed), 11)
    own_keys = jax.random.split(jax.random.fold_in(key_of[10], part), 11)
    return {
        "tokens": draw_tokens(jax.random.fold_in(jax.random.fold_in(key_of[10], part), 71), part),
        "norm_gain": jnp.clip(1.0 + 0.18 * jax.random.normal(key_of[1], (D,), jnp.float32), 0.1, 1.9),
        "block_mask": draw_block_mask(jax.random.fold_in(jax.random.fold_in(key_of[10], part), 71), part),
        "w_query": draw_w_query(jax.random.fold_in(key_of[10], 71), part),
        "w_key": draw_w_key(jax.random.fold_in(key_of[10], 71), part),
        "w_value": scatter_about(key_of[5], (D, D), D ** -0.5, 0.1875, ((0, 2), (1, 2))),
        "w_out": scatter_about(key_of[6], (D, D), D ** -0.5, 0.1875, ((0, 2), (1, 2))),
        "w_up": scatter_about(key_of[7], (D, FF), D ** -0.5, 0.1875, ((0, 2), (1, 2))),
        "w_down": scatter_about(key_of[8], (FF, D), FF ** -0.5, 0.125, ((0, 2), (1, 2))),
        "conv_weight": scatter_about(key_of[9], (KERNEL, D), KERNEL ** -0.5, 2.5, ((1, 2),), jnp.float32),
    }


def rms_norm(tokens, norm_gain):
    values = tokens.astype(jnp.float32)
    square = lax.optimization_barrier(jnp.mean(values * values, axis=-1, keepdims=True))
    return (values * lax.rsqrt(square + 1e-05) * norm_gain).astype(jnp.bfloat16)

def reference(tokens, norm_gain, block_mask, w_query, w_key, w_value, w_out, w_up, w_down, conv_weight):
    normed = rms_norm(tokens, norm_gain)
    flat = normed.reshape(FRAMES * DANCERS, D)
    queries = jnp.dot(flat, w_query, preferred_element_type=jnp.float32).astype(jnp.bfloat16)
    keys = jnp.dot(flat, w_key, preferred_element_type=jnp.float32).astype(jnp.bfloat16)
    values = jnp.dot(flat, w_value, preferred_element_type=jnp.float32).astype(jnp.bfloat16)
    window_tokens = FRAME_DEV * DANCERS

    def split_heads(array):
        return array.reshape(N_TM, window_tokens, HEADS, HEAD_DIM).transpose(0, 2, 1, 3)
    blocks = jnp.arange(DANCERS) // DAN_DEV
    chooser = (blocks[:, None] == jnp.arange(N_CTX)[None, :]).astype(jnp.float32)

    def window(inputs):
        query_w, key_w, value_w, mask_w = inputs
        dancer_mask = jnp.dot(jnp.dot(chooser, mask_w.astype(jnp.float32)), chooser.T)
        allowed = jnp.tile(dancer_mask, (FRAME_DEV, FRAME_DEV))

        def one_head(head_inputs):
            head_q, head_k, head_v = head_inputs
            scores = jnp.dot(head_q, head_k.T, preferred_element_type=jnp.float32) * 0.125
            scores = jnp.where(allowed > 0, scores, -1e+30)
            peak = lax.optimization_barrier(jnp.max(scores, axis=-1, keepdims=True))
            expo = jnp.exp(scores - peak) * allowed
            total = lax.optimization_barrier(jnp.sum(expo, axis=-1, keepdims=True))
            probs = expo.astype(jnp.bfloat16)
            mixed = jnp.dot(probs, head_v, preferred_element_type=jnp.float32)
            return mixed / total
        return lax.map(one_head, (query_w, key_w, value_w))
    attended = lax.map(window, (split_heads(queries), split_heads(keys), split_heads(values), block_mask))
    attended = attended.transpose(0, 2, 1, 3).reshape(FRAMES * DANCERS, D).astype(jnp.bfloat16)
    hidden = jnp.dot(flat, w_up, preferred_element_type=jnp.float32)
    activated = jax.nn.gelu(hidden, approximate=True).astype(jnp.bfloat16)
    branches = jnp.dot(attended, w_out, preferred_element_type=jnp.float32)
    branches = branches + jnp.dot(activated, w_down, preferred_element_type=jnp.float32)
    padded = jnp.pad(normed.astype(jnp.float32), ((2, 2), (0, 0), (0, 0)))
    convolved = jnp.zeros((FRAMES, DANCERS, D), jnp.float32)
    for offset in range(KERNEL):
        convolved = convolved + conv_weight[offset] * padded[offset:offset + FRAMES]
    total_out = tokens.astype(jnp.float32) + branches.reshape(FRAMES, DANCERS, D) + convolved
    return total_out.astype(jnp.bfloat16)
```

```python
import functools

import jax
import jax.numpy as jnp
from jax import lax
from jax.experimental import pallas as pl
from jax.experimental.pallas import tpu as pltpu
from jax.sharding import PartitionSpec as P

HEAD_DIM = 64
KERNEL = 5


def from_behind(value, axis, steps):
    count = lax.axis_size(axis)
    first, last = (max(0, -steps), min(count, count - steps))
    return lax.ppermute(value, axis, [(source, source + steps) for source in range(first, last)])


def rms_norm(tokens, norm_gain):
    values = tokens.astype(jnp.float32)
    square = jnp.mean(values * values, axis=-1, keepdims=True)
    return (values * lax.rsqrt(square + 1e-05) * norm_gain).astype(jnp.bfloat16)


def on_device(
    tokens, norm_gain, block_mask, w_query, w_key, w_value, w_out, w_up, w_down, conv_weight
):
    frames_here, dancers_here, width = tokens.shape
    rows_here = frames_here * dancers_here
    normed_grid = rms_norm(tokens, norm_gain)
    normed = normed_grid.reshape(rows_here, width)
    pieces = (
        lax.all_gather(w_query, "tm", axis=0, tiled=True),
        lax.all_gather(w_key, "tm", axis=0, tiled=True),
        lax.all_gather(w_value, "tm", axis=0, tiled=True),
        lax.all_gather(w_up, "tm", axis=0, tiled=True),
    )
    query_sum, key_sum, value_sum, hidden = tuple(
        (jnp.dot(normed, piece_one, preferred_element_type=jnp.float32) for piece_one in pieces)
    )
    local_heads = query_sum.shape[1] // HEAD_DIM
    queries = query_sum.astype(jnp.bfloat16).reshape(rows_here, local_heads, HEAD_DIM)
    key_grid = key_sum.astype(jnp.bfloat16).reshape(
        frames_here, dancers_here, local_heads * HEAD_DIM
    )
    value_grid = value_sum.astype(jnp.bfloat16).reshape(
        frames_here, dancers_here, local_heads * HEAD_DIM
    )
    mask_row = block_mask[0, 0].astype(jnp.float32)
    cycle_blocks = mask_row.shape[0]
    key_piece = lax.all_gather(key_grid, "ctx", axis=1, tiled=True)
    value_piece = lax.all_gather(value_grid, "ctx", axis=1, tiled=True)
    count = key_piece.shape[1]
    block_ids = jnp.arange(count) // dancers_here
    picker = (block_ids[:, None] == jnp.arange(cycle_blocks)[None, :]).astype(jnp.float32)
    allowed_dancers = jnp.dot(picker, mask_row)
    peak_old = jnp.full((local_heads, rows_here), -1e30, jnp.float32)
    key_rows = key_piece.reshape(frames_here * count, local_heads, HEAD_DIM)
    value_rows = value_piece.reshape(frames_here * count, local_heads, HEAD_DIM)
    allowed = jnp.tile(allowed_dancers, frames_here)
    scores = (
        jnp.einsum("qhd,khd->hqk", queries, key_rows, preferred_element_type=jnp.float32) * 0.125
    )
    scores = jnp.where(allowed[None, None, :] > 0, scores, -1e30)
    peak_new = jnp.maximum(peak_old, jnp.max(scores, axis=-1))
    expo = jnp.exp(scores - peak_new[:, :, None]) * allowed[None, None, :]
    total_new = jnp.sum(expo, axis=-1)
    probs = expo.astype(jnp.bfloat16)
    mixed_new = jnp.einsum("hqk,khd->hqd", probs, value_rows, preferred_element_type=jnp.float32)
    attended = (
        (mixed_new / total_new[:, :, None])
        .transpose(1, 0, 2)
        .reshape(rows_here, local_heads * HEAD_DIM)
        .astype(jnp.bfloat16)
    )
    activated = jax.nn.gelu(hidden, approximate=True).astype(jnp.bfloat16)
    out_full, down_full = (
        lax.all_gather(w_out, "tm", axis=1, tiled=True),
        lax.all_gather(w_down, "tm", axis=1, tiled=True),
    )
    branches = jnp.dot(attended, out_full, preferred_element_type=jnp.float32)
    branches = branches + jnp.dot(activated, down_full, preferred_element_type=jnp.float32)
    mine = lax.psum_scatter(
        branches.astype(jnp.bfloat16), "tp", scatter_dimension=1, tiled=True
    ).astype(jnp.float32)
    features_here = mine.shape[1]
    first_feature = lax.axis_index("tp") * features_here
    normed_cols = lax.dynamic_slice_in_dim(normed_grid, first_feature, features_here, 2)
    padded = jnp.pad(normed_cols.astype(jnp.float32), ((4, 4), (0, 0), (0, 0)))
    extended = jnp.zeros((frames_here + 4, dancers_here, features_here), jnp.float32)
    for offset in range(KERNEL):
        extended = extended + conv_weight[offset] * padded[offset : offset + frames_here + 4]
    convolved = extended[2 : frames_here + 2]
    from_before = from_behind(extended[frames_here + 2 :], "tm", 1)
    from_after = from_behind(extended[0:2], "tm", -1)
    convolved = convolved.at[0:2].add(from_before)
    convolved = convolved.at[frames_here - 2 :].add(from_after)
    token_cols = lax.dynamic_slice_in_dim(tokens, first_feature, features_here, 2).astype(
        jnp.float32
    )
    result = token_cols + mine.reshape(frames_here, dancers_here, features_here) + convolved
    return result.astype(jnp.bfloat16)


MESH = pl.DeviceIdType.MESH
N_LINE = 4


def normalised(values, gain):
    values = values.astype(jnp.float32)
    square = jnp.mean(values * values, axis=-1, keepdims=True)
    return (values * lax.rsqrt(square + 1e-05) * gain).astype(jnp.bfloat16)


def layer_kernel(
    frame,
    mask_hbm,
    tokens_hbm,
    gain_hbm,
    conv_hbm,
    wq_ref,
    wk_ref,
    wv_ref,
    wup_ref,
    wout_ref,
    wdown_ref,
    out_ref,
    mask_ref,
    gain_ref,
    conv_ref,
    tok_raw,
    normed,
    halo,
    halo_normed,
    bias,
    w_in,
    w_back,
    qkv,
    feats,
    mine,
    summed,
    arrived,
    extended,
    local_sem,
    tok_send,
    tok_recv,
    fwd_send,
    fwd_recv,
    bias_send,
    bias_recv,
    x_send,
    x_recv,
    y_send,
    y_recv,
    back_send,
    back_recv,
    over_send,
    over_recv,
    sib_send,
    sib_recv,
    halo_sem,
    act_send,
    act_recv,
    att_send,
    att_recv,
    red_send,
    red_recv,
):
    g = lax.axis_index("groups")
    c = lax.axis_index("ctx")
    i = lax.axis_index("tm")
    j = lax.axis_index("tp")
    frames, dancers, width = tokens_hbm.shape
    rows = frames * dancers
    half_frames = frames // 2
    depth = wq_ref.shape[0]
    part = depth // 2
    hw = wq_ref.shape[1] // N_LINE
    fw = wup_ref.shape[1] // N_LINE
    cols = out_ref.shape[2]
    heads = hw // HEAD_DIM
    to_x = {"tm": 1 - i}
    to_y = {"groups": 1 - g}
    to_tp = {"tp": 1 - j}

    is_end = lax.rem(lax.div(c + 1, 2), 2) == 0
    e = 1 - lax.rem(lax.div(c + 1, 2), 2)
    is_mid = jnp.logical_not(is_end)
    mate = c + 1 - 2 * lax.rem(c, 2)
    cross = lax.rem(c + 2, N_LINE)
    opp = N_LINE - 1 - c
    first = e * mate + (1 - e) * opp
    second = e * opp + (1 - e) * mate
    slot_first = 2 * (1 - e)
    slot_second = 2 * e
    early = j == i
    late = j != i

    barrier = pltpu.get_barrier_semaphore()
    peers = [to_x, to_y, to_tp, {"ctx": mate}, {"ctx": cross}, {"ctx": opp}, {"tm": 1 - i, "tp": 1 - j}]
    for peer in peers:
        pl.semaphore_signal(barrier, inc=1, device_id=peer, device_id_type=MESH)

    def rows_at(start, size):
        return pl.ds(pl.multiple_of(start, 16), size)

    def cols_at(start, size):
        return pl.ds(pl.multiple_of(start, 128), size)

    own = rows_at(c * rows, rows)
    tok_copy = pltpu.make_async_copy(tokens_hbm, tok_raw.at[c], local_sem.at[6])
    mask_copy = pltpu.make_async_copy(mask_hbm, mask_ref, local_sem.at[9])
    gain_copy = pltpu.make_async_copy(gain_hbm, gain_ref, local_sem.at[7])
    conv_copy = pltpu.make_async_copy(conv_hbm, conv_ref, local_sem.at[8])
    own_depth = rows_at(i * depth, depth)
    in_copies = [
        pltpu.make_async_copy(
            ref.at[:, cols_at(c * hw, hw)],
            w_in.at[own_depth, k * hw : (k + 1) * hw],
            local_sem.at[k],
        )
        for k, ref in enumerate((wq_ref, wk_ref, wv_ref))
    ]
    in_copies.append(
        pltpu.make_async_copy(
            wup_ref.at[:, cols_at(c * fw, fw)],
            w_in.at[own_depth, 3 * hw : 3 * hw + fw],
            local_sem.at[3],
        )
    )
    out_src = wout_ref.at[rows_at(c * hw, hw), :]
    down_src = wdown_ref.at[rows_at(c * fw, fw), :]
    out_rows = rows_at(j * hw, hw)
    down_rows = rows_at(2 * hw + j * fw, fw)
    back_copies = [
        pltpu.make_async_copy(out_src, w_back.at[out_rows], local_sem.at[4]),
        pltpu.make_async_copy(down_src, w_back.at[down_rows], local_sem.at[5]),
    ]
    mask_copy.start()
    tok_copy.start()
    gain_copy.start()
    for copy in in_copies:
        copy.start()
    conv_copy.start()

    @pl.when(early)
    def _():
        for copy in back_copies:
            copy.start()

    sends = []

    def remote(source, target, send, recv, peer):
        return pltpu.make_async_remote_copy(
            src_ref=source,
            dst_ref=target,
            send_sem=send,
            recv_sem=recv,
            device_id=peer,
            device_id_type=MESH,
        )

    def launch(copies, condition=None):
        if condition is None:
            for copy in copies:
                copy.start()
        else:

            @pl.when(condition)
            def _():
                for copy in copies:
                    copy.start()

        sends.append((condition, copies))

    def token_half(block, half):
        return tok_raw.at[block, pl.ds(half * half_frames, half_frames)]

    own_half = tokens_hbm.at[pl.ds(j * half_frames, half_frames)]

    def token_copy(slot, peer, send):
        return remote(own_half, token_half(c, j), tok_send.at[send], tok_recv.at[slot], peer)

    def token_wait(block, slot):
        half = token_half(block, j)
        remote(half, half, tok_send.at[0], tok_recv.at[slot], to_tp).wait_recv()

    pl.semaphore_wait(barrier, len(peers))
    launch(
        [
            token_copy(2, {"ctx": opp}, 0),
            token_copy(0, {"ctx": mate}, 1),
            token_copy(1, {"ctx": cross}, 2),
        ],
        is_end,
    )
    launch([token_copy(2, {"ctx": opp}, 0), token_copy(0, {"ctx": mate}, 1)], is_mid)

    def in_slices(half, owner):
        base = owner * depth + half * part
        out = []
        for k in range(3):
            out.append(w_in.at[rows_at(base, part), k * hw : (k + 1) * hw])
        for k in range(2):
            out.append(w_in.at[rows_at(base + k * (part // 2), part // 2), 3 * hw : 3 * hw + fw])
        return out

    in_sources = [
        ref.at[rows_at(g * part, part), cols_at(c * hw, hw)] for ref in (wq_ref, wk_ref, wv_ref)
    ]
    for k in range(2):
        in_sources.append(
            wup_ref.at[rows_at(g * part + k * (part // 2), part // 2), cols_at(c * fw, fw)]
        )
    x_out = [
        remote(source, ref, x_send.at[k], x_recv.at[k], to_x)
        for k, (source, ref) in enumerate(zip(in_sources, in_slices(g, i)))
    ]
    x_in = [
        remote(ref, ref, x_send.at[k], x_recv.at[k], to_x)
        for k, ref in enumerate(in_slices(g, 1 - i))
    ]
    y_out = [
        remote(ref, ref, y_send.at[k], y_recv.at[k], to_y)
        for k, ref in enumerate(in_slices(g, 1 - i))
    ]
    y_in = [
        remote(ref, ref, y_send.at[k], y_recv.at[k], to_y)
        for k, ref in enumerate(in_slices(1 - g, 1 - i))
    ]
    launch(x_out)

    half_out = hw // 2
    over_peer = {"tm": 1 - i, "tp": i}

    def out_half(core, half):
        return w_back.at[rows_at(core * hw + half * half_out, half_out)]

    def down_whole(core):
        return w_back.at[rows_at(2 * hw + core * fw, fw)]

    launch(
        [
            remote(
                wout_ref.at[rows_at(c * hw + g * half_out, half_out), :],
                out_half(j, g),
                back_send.at[0],
                back_recv.at[j],
                over_peer,
            ),
            remote(down_src, down_whole(j), back_send.at[1], back_recv.at[2 + j], over_peer),
        ]
    )
    back_in = [
        remote(out_half(core, g), out_half(core, g), back_send.at[0], back_recv.at[core], over_peer)
        for core in range(2)
    ]
    down_in = [
        remote(down_whole(core), down_whole(core), back_send.at[1], back_recv.at[2 + core], over_peer)
        for core in range(2)
    ]
    over_out = [
        remote(out_half(core, g), out_half(core, g), over_send.at[core], over_recv.at[core], to_y)
        for core in range(2)
    ]
    over_in = [
        remote(
            out_half(core, 1 - g), out_half(core, 1 - g), over_send.at[core], over_recv.at[core], to_y
        )
        for core in range(2)
    ]
    sib_out = [
        remote(out_src, w_back.at[out_rows], sib_send.at[0], sib_recv.at[0], to_tp),
        remote(down_src, w_back.at[down_rows], sib_send.at[1], sib_recv.at[1], to_tp),
    ]
    launch(sib_out, late)
    their_out = w_back.at[rows_at((1 - j) * hw, hw)]
    their_down = w_back.at[rows_at(2 * hw + (1 - j) * fw, fw)]
    sib_in = [
        remote(their_out, their_out, sib_send.at[0], sib_recv.at[0], to_tp),
        remote(their_down, their_down, sib_send.at[1], sib_recv.at[1], to_tp),
    ]
    halo_copy = remote(
        tokens_hbm.at[pl.ds((1 - i) * (frames - 8), 8)],
        halo,
        halo_sem.at[0],
        halo_sem.at[1],
        to_x,
    )
    launch([halo_copy])
    mask_copy.wait()
    row_ids = lax.broadcasted_iota(jnp.int32, (8, 128), 0)
    tile = jnp.zeros((8, 128), jnp.float32)
    for block in range(N_LINE):
        term = (mask_ref[0, block].astype(jnp.float32) - 1.0) * 1e30
        tile = jnp.where(row_ids == block, term, tile)
    bias[c] = tile

    bias_out, bias_in = [], []
    for slot, peer in enumerate((mate, cross, opp)):
        bias_out.append(
            remote(bias.at[c], bias.at[c], bias_send.at[slot], bias_recv.at[slot], {"ctx": peer})
        )
        bias_in.append(
            remote(
                bias.at[peer], bias.at[peer], bias_send.at[slot], bias_recv.at[slot], {"ctx": peer}
            )
        )
    launch(bias_out)

    gain_copy.wait()
    gain = gain_ref[...]

    def norm_block(block):
        at = rows_at(block * rows, rows)
        normed[at, :] = normalised(tok_raw[block].reshape(rows, width), gain)

    def pass_on(index):
        x_in[index].wait_recv()
        launch([y_out[index]])

    def share(block, slot):
        token_wait(block, slot)
        launch(
            [remote(token_half(block, j), token_half(block, j), fwd_send.at[slot], fwd_recv.at[slot], to_tp)]
        )

    def settle(block, slot):
        half = token_half(block, 1 - j)
        remote(half, half, fwd_send.at[slot], fwd_recv.at[slot], to_tp).wait_recv()
        norm_block(block)

    def project(block):
        at = rows_at(block * rows, rows)
        qkv[at, :] = jnp.dot(
            normed[at, :], w_in[:, 0 : 3 * hw], preferred_element_type=jnp.float32
        ).astype(jnp.bfloat16)

    order = [second, cross, first, c]
    att_cols = cols_at(j * hw, hw)
    act_cols = cols_at(2 * hw + j * fw, fw)

    def feature_copy(index, columns, send, recv):
        ref = feats.at[rows_at(order[index] * rows, rows), columns]
        return remote(ref, ref, send.at[index], recv.at[index], to_tp)

    def feed(index):
        at = rows_at(order[index] * rows, rows)
        hidden = jnp.dot(
            normed[at, :], w_in[:, 3 * hw : 3 * hw + fw], preferred_element_type=jnp.float32
        )
        feats[at, act_cols] = jax.nn.gelu(hidden, approximate=True).astype(jnp.bfloat16)
        launch([feature_copy(index, act_cols, act_send, act_recv)])

    def attend(index):
        block = order[index]
        at = rows_at(block * rows, rows)
        marks = bias[block]
        mark = jnp.concatenate([marks[k : k + 1, :] for k in range(N_LINE)], axis=1)
        outs = []
        for head in range(heads):
            low = head * HEAD_DIM
            query = qkv[at, low : low + HEAD_DIM]
            key = qkv[:, hw + low : hw + low + HEAD_DIM]
            value = qkv[:, 2 * hw + low : 2 * hw + low + HEAD_DIM]
            scores = lax.dot_general(
                query, key, (((1,), (1,)), ((), ())), preferred_element_type=jnp.float32
            )
            scores = scores * 0.125 + mark
            peak = jnp.max(scores, axis=-1, keepdims=True)
            expo = jnp.exp(scores - peak)
            total = jnp.sum(expo, axis=-1, keepdims=True)
            mixed = jnp.dot(
                expo.astype(jnp.bfloat16), value, preferred_element_type=jnp.float32
            )
            outs.append(mixed / total)
        feats[at, att_cols] = jnp.concatenate(outs, axis=1).astype(jnp.bfloat16)
        launch([feature_copy(index, att_cols, att_send, att_recv)])

    other_att = cols_at((1 - j) * hw, hw)
    other_act = cols_at(2 * hw + (1 - j) * fw, fw)

    def arrive(slot, send, peer):
        copies = []
        for half in range(2):
            at = slice(half * (rows // 2), (half + 1) * (rows // 2))
            copies.append(
                remote(
                    summed.at[send, at],
                    arrived.at[slot, at],
                    red_send.at[2 * send + half],
                    red_recv.at[2 * slot + half],
                    peer,
                )
            )
        return copies

    def wait_arrived(slot, halves=(0, 1)):
        copies = arrive(slot, 0, to_tp)
        for half in halves:
            copies[half].wait_recv()

    end_slots = [0, 1, 2]

    def product(index):
        feature_copy(index, other_att, att_send, att_recv).wait_recv()
        feature_copy(index, other_act, act_send, act_recv).wait_recv()
        at = rows_at(order[index] * rows, rows)
        return jnp.dot(feats[at, :], w_back[...], preferred_element_type=jnp.float32)

    def emit(index):
        value = product(index)
        if index == 3:
            mine[2] = value
            return

        @pl.when(is_end)
        def _():
            summed[index] = value.astype(jnp.bfloat16)
            for copy in arrive(end_slots[index], index, {"ctx": mate}):
                copy.start()

        @pl.when(is_mid)
        def _():
            if index == 0:
                summed[0] = value.astype(jnp.bfloat16)
                for copy in arrive(2, 0, {"ctx": mate}):
                    copy.start()
            else:
                mine[index - 1] = value

    def relay(index):
        peer = {"ctx": cross} if index == 1 else {"ctx": opp}
        copies = arrive(3, index, peer)
        for half in range(2):
            at = slice(half * (rows // 2), (half + 1) * (rows // 2))
            wait_arrived(index - 1, (half,))
            summed[index, at] = (
                mine[index - 1, at] + arrived[index - 1, at].astype(jnp.float32)
            ).astype(jnp.bfloat16)
            copies[half].start()

    def emit_all():
        for index in range(3):
            emit(index)

        @pl.when(is_mid)
        def _():
            relay(1)

        emit(3)

        @pl.when(is_mid)
        def _():
            relay(2)

    tok_copy.wait()
    norm_block(c)
    pass_on(0)
    pass_on(1)
    token_wait(first, slot_first)
    relayed = remote(
        token_half(opp, j), token_half(opp, j), tok_send.at[3], tok_recv.at[1], {"ctx": mate}
    )
    launch([relayed], is_mid)
    launch(
        [
            remote(
                token_half(first, j),
                token_half(first, j),
                fwd_send.at[slot_first],
                fwd_recv.at[slot_first],
                to_tp,
            )
        ]
    )
    pass_on(2)
    settle(first, slot_first)
    pass_on(3)
    share(second, slot_second)
    pass_on(4)
    settle(second, slot_second)
    for copy in y_in[:3]:
        copy.wait_recv()
    for copy in in_copies:
        copy.wait()
    project(c)
    share(cross, 1)
    project(first)
    project(second)
    settle(cross, 1)
    project(cross)

    @pl.when(late)
    def _():
        for core in range(2):
            back_in[core].wait_recv()
            over_out[core].start()

    for copy in bias_in:
        copy.wait_recv()
    attend(0)
    for copy in y_in[3:]:
        copy.wait_recv()
    feed(0)
    attend(1)
    feed(1)

    @pl.when(early)
    def _():
        for copy in back_copies:
            copy.wait()
        for copy in sib_in:
            copy.wait_recv()
        emit(0)

    feed(2)
    feed(3)
    attend(2)

    @pl.when(early)
    def _():
        emit(1)

    attend(3)

    @pl.when(early)
    def _():
        emit(2)

        @pl.when(is_mid)
        def _():
            relay(1)

        emit(3)

        @pl.when(is_mid)
        def _():
            relay(2)

    conv_copy.wait()
    halo_copy.wait_recv()
    halo_normed[...] = normalised(halo[...].reshape(16, width), gain)
    my_cols = cols_at(j * cols, cols)
    edge = halo_normed[:, my_cols].astype(jnp.float32)
    reach = KERNEL // 2
    extended[0:8, :] = jnp.where(i == 1, edge[8:16], 0.0)
    extended[8 : 8 + rows, :] = normed[own, my_cols].astype(jnp.float32)
    extended[8 + rows : 16 + rows, :] = jnp.where(i == 0, edge[0:8], 0.0)
    base = tok_raw[c, :, :, my_cols].reshape(rows, cols).astype(jnp.float32)
    for tap in range(KERNEL):
        shift = 8 + (tap - reach) * frame
        base = base + conv_ref[tap : tap + 1, :] * extended[shift : shift + rows, :]
    mine[3] = base

    @pl.when(late)
    def _():
        for copy in over_in + down_in:
            copy.wait_recv()
        emit_all()

    wait_arrived(2)
    base = mine[3] + mine[2] + arrived[2].astype(jnp.float32)
    wait_arrived(3)
    whole = (base + arrived[3].astype(jnp.float32)).astype(out_ref.dtype)
    out_ref[...] = whole.reshape(frames, dancers, cols)

    @pl.when(late)
    def _():
        for copy in over_out:
            copy.wait_send()

    for index in range(3):
        for copy in arrive(2, index, {"ctx": mate}):
            copy.wait_send()
    for condition, copies in sends:
        if condition is None:
            for copy in copies:
                copy.wait_send()
        else:

            @pl.when(condition)
            def _(copies=copies):
                for copy in copies:
                    copy.wait_send()


def in_one_kernel(
    tokens, norm_gain, block_mask, w_query, w_key, w_value, w_out, w_up, w_down, conv_weight
):
    frames_here, dancers_here, width = tokens.shape
    rows = frames_here * dancers_here
    cols = w_out.shape[1]
    hw = w_query.shape[1] // N_LINE
    fw = w_up.shape[1] // N_LINE
    depth = w_query.shape[0]
    every = N_LINE * rows
    bf16, f32 = jnp.bfloat16, jnp.float32
    vmem = pl.BlockSpec(memory_space=pltpu.VMEM)
    hbm = pl.BlockSpec(memory_space=pltpu.HBM)
    dma = pltpu.SemaphoreType.DMA
    out = pl.pallas_call(
        functools.partial(layer_kernel, dancers_here),
        out_shape=jax.ShapeDtypeStruct((frames_here, dancers_here, cols), bf16),
        in_specs=[hbm] * 10,
        out_specs=vmem,
        scratch_shapes=[
            pltpu.SMEM((1, N_LINE), jnp.int32),
            pltpu.VMEM((1, width), f32),
            pltpu.VMEM(conv_weight.shape, f32),
            pltpu.VMEM((N_LINE,) + tokens.shape, bf16),
            pltpu.VMEM((every, width), bf16),
            pltpu.VMEM((16 // dancers_here, dancers_here, width), bf16),
            pltpu.VMEM((16, width), bf16),
            pltpu.VMEM((N_LINE, 8, 128), f32),
            pltpu.VMEM((2 * depth, 3 * hw + fw), bf16),
            pltpu.VMEM((2 * hw + 2 * fw, cols), bf16),
            pltpu.VMEM((every, 3 * hw), bf16),
            pltpu.VMEM((every, 2 * hw + 2 * fw), bf16),
            pltpu.VMEM((4, rows, cols), f32),
            pltpu.VMEM((3, rows, cols), bf16),
            pltpu.VMEM((4, rows, cols), bf16),
            pltpu.VMEM((rows + 16, cols), f32),
            dma((10,)),
            dma((4,)),
            dma((3,)),
            dma((3,)),
            dma((3,)),
            dma((3,)),
            dma((3,)),
            dma((5,)),
            dma((5,)),
            dma((5,)),
            dma((5,)),
            dma((2,)),
            dma((4,)),
            dma((2,)),
            dma((2,)),
            dma((2,)),
            dma((2,)),
            dma((2,)),
            dma((4,)),
            dma((4,)),
            dma((4,)),
            dma((4,)),
            dma((6,)),
            dma((8,)),
        ],
        compiler_params=pltpu.CompilerParams(
            collective_id=0, has_side_effects=True, vmem_limit_bytes=40 << 20
        ),
    )(
        *[
            pltpu.with_memory_space_constraint(operand, pltpu.HBM)
            for operand in (
                block_mask[0],
                tokens,
                norm_gain[None],
                conv_weight,
                w_query,
                w_key,
                w_value,
                w_up,
                w_out,
                w_down,
            )
        ]
    )
    return out


def solution(mesh):
    def body(tokens, norm_gain, block_mask, w_query, *rest):
        pairs = all(mesh.shape[axis] == 2 for axis in ("groups", "tm", "tp"))
        line = mesh.shape["ctx"] == N_LINE
        rows = tokens.shape[0] * tokens.shape[1]
        split = w_query.shape[1] == 128 * N_LINE and tokens.shape[1] * (KERNEL // 2) <= 8
        if pairs and line and split and rows == 128 and tokens.shape[1] == 2:
            return in_one_kernel(tokens, norm_gain, block_mask, w_query, *rest)
        return on_device(tokens, norm_gain, block_mask, w_query, *rest)

    placed = (
        P(("groups", "tm"), "ctx", None),
        P(),
        P(("groups", "tm"), "ctx", None),
        P("tm", "tp"),
        P("tm", "tp"),
        P("tm", "tp"),
        P("tp", "tm"),
        P("tm", "tp"),
        P("tp", "tm"),
        P(None, "tp"),
    )
    return jax.shard_map(
        body,
        mesh=mesh,
        in_specs=placed,
        out_specs=P(("groups", "tm"), "ctx", "tp"),
        check_vma=False,
    )
```

```python
import functools

import jax
import jax.numpy as jnp
from jax import lax
from jax.experimental import pallas as pl
from jax.experimental.pallas import tpu as pltpu
from jax.sharding import PartitionSpec as P

HEAD_DIM = 64
KERNEL = 5


def from_behind(value, axis, steps):
    count = lax.axis_size(axis)
    first, last = (max(0, -steps), min(count, count - steps))
    return lax.ppermute(value, axis, [(source, source + steps) for source in range(first, last)])


def rms_norm(tokens, norm_gain):
    values = tokens.astype(jnp.float32)
    square = jnp.mean(values * values, axis=-1, keepdims=True)
    return (values * lax.rsqrt(square + 1e-05) * norm_gain).astype(jnp.bfloat16)


def on_device(
    tokens, norm_gain, block_mask, w_query, w_key, w_value, w_out, w_up, w_down, conv_weight
):
    frames_here, dancers_here, width = tokens.shape
    rows_here = frames_here * dancers_here
    normed_grid = rms_norm(tokens, norm_gain)
    normed = normed_grid.reshape(rows_here, width)
    pieces = (
        lax.all_gather(w_query, "tm", axis=0, tiled=True),
        lax.all_gather(w_key, "tm", axis=0, tiled=True),
        lax.all_gather(w_value, "tm", axis=0, tiled=True),
        lax.all_gather(w_up, "tm", axis=0, tiled=True),
    )
    query_sum, key_sum, value_sum, hidden = tuple(
        (jnp.dot(normed, piece_one, preferred_element_type=jnp.float32) for piece_one in pieces)
    )
    local_heads = query_sum.shape[1] // HEAD_DIM
    queries = query_sum.astype(jnp.bfloat16).reshape(rows_here, local_heads, HEAD_DIM)
    key_grid = key_sum.astype(jnp.bfloat16).reshape(
        frames_here, dancers_here, local_heads * HEAD_DIM
    )
    value_grid = value_sum.astype(jnp.bfloat16).reshape(
        frames_here, dancers_here, local_heads * HEAD_DIM
    )
    mask_row = block_mask[0, 0].astype(jnp.float32)
    cycle_blocks = mask_row.shape[0]
    key_piece = lax.all_gather(key_grid, "ctx", axis=1, tiled=True)
    value_piece = lax.all_gather(value_grid, "ctx", axis=1, tiled=True)
    count = key_piece.shape[1]
    block_ids = jnp.arange(count) // dancers_here
    picker = (block_ids[:, None] == jnp.arange(cycle_blocks)[None, :]).astype(jnp.float32)
    allowed_dancers = jnp.dot(picker, mask_row)
    peak_old = jnp.full((local_heads, rows_here), -1e30, jnp.float32)
    key_rows = key_piece.reshape(frames_here * count, local_heads, HEAD_DIM)
    value_rows = value_piece.reshape(frames_here * count, local_heads, HEAD_DIM)
    allowed = jnp.tile(allowed_dancers, frames_here)
    scores = (
        jnp.einsum("qhd,khd->hqk", queries, key_rows, preferred_element_type=jnp.float32) * 0.125
    )
    scores = jnp.where(allowed[None, None, :] > 0, scores, -1e30)
    peak_new = jnp.maximum(peak_old, jnp.max(scores, axis=-1))
    expo = jnp.exp(scores - peak_new[:, :, None]) * allowed[None, None, :]
    total_new = jnp.sum(expo, axis=-1)
    probs = expo.astype(jnp.bfloat16)
    mixed_new = jnp.einsum("hqk,khd->hqd", probs, value_rows, preferred_element_type=jnp.float32)
    attended = (
        (mixed_new / total_new[:, :, None])
        .transpose(1, 0, 2)
        .reshape(rows_here, local_heads * HEAD_DIM)
        .astype(jnp.bfloat16)
    )
    activated = jax.nn.gelu(hidden, approximate=True).astype(jnp.bfloat16)
    out_full, down_full = (
        lax.all_gather(w_out, "tm", axis=1, tiled=True),
        lax.all_gather(w_down, "tm", axis=1, tiled=True),
    )
    branches = jnp.dot(attended, out_full, preferred_element_type=jnp.float32)
    branches = branches + jnp.dot(activated, down_full, preferred_element_type=jnp.float32)
    mine = lax.psum_scatter(
        branches.astype(jnp.bfloat16), "tp", scatter_dimension=1, tiled=True
    ).astype(jnp.float32)
    features_here = mine.shape[1]
    first_feature = lax.axis_index("tp") * features_here
    normed_cols = lax.dynamic_slice_in_dim(normed_grid, first_feature, features_here, 2)
    padded = jnp.pad(normed_cols.astype(jnp.float32), ((4, 4), (0, 0), (0, 0)))
    extended = jnp.zeros((frames_here + 4, dancers_here, features_here), jnp.float32)
    for offset in range(KERNEL):
        extended = extended + conv_weight[offset] * padded[offset : offset + frames_here + 4]
    convolved = extended[2 : frames_here + 2]
    from_before = from_behind(extended[frames_here + 2 :], "tm", 1)
    from_after = from_behind(extended[0:2], "tm", -1)
    convolved = convolved.at[0:2].add(from_before)
    convolved = convolved.at[frames_here - 2 :].add(from_after)
    token_cols = lax.dynamic_slice_in_dim(tokens, first_feature, features_here, 2).astype(
        jnp.float32
    )
    result = token_cols + mine.reshape(frames_here, dancers_here, features_here) + convolved
    return result.astype(jnp.bfloat16)


MESH = pl.DeviceIdType.MESH
N_LINE = 4


def normalised(values, gain):
    values = values.astype(jnp.float32)
    square = jnp.mean(values * values, axis=-1, keepdims=True)
    return (values * lax.rsqrt(square + 1e-05) * gain).astype(jnp.bfloat16)


PIECES = 4


def layer_kernel(
    frame,
    mask_hbm,
    tokens_hbm,
    gain_hbm,
    conv_hbm,
    wq_ref,
    wk_ref,
    wv_ref,
    wup_ref,
    wout_ref,
    wdown_ref,
    out_ref,
    mask_ref,
    gain_ref,
    conv_ref,
    tok_raw,
    normed,
    halo,
    halo_normed,
    bias,
    w_in,
    w_back,
    qkv,
    feats,
    mine,
    summed,
    arrived,
    extended,
    local_sem,
    tok_send,
    tok_recv,
    fwd_send,
    fwd_recv,
    bias_send,
    bias_recv,
    x_send,
    x_recv,
    y_send,
    y_recv,
    back_send,
    back_recv,
    over_send,
    over_recv,
    sib_send,
    sib_recv,
    halo_sem,
    act_send,
    act_recv,
    att_send,
    att_recv,
    red_send,
    red_recv,
):
    g = lax.axis_index("groups")
    c = lax.axis_index("ctx")
    i = lax.axis_index("tm")
    j = lax.axis_index("tp")
    frames, dancers, width = tokens_hbm.shape
    rows = frames * dancers
    half_frames = frames // 2
    depth = wq_ref.shape[0]
    part = depth // 2
    hw = wq_ref.shape[1] // N_LINE
    fw = wup_ref.shape[1] // N_LINE
    cols = out_ref.shape[2]
    heads = hw // HEAD_DIM
    to_x = {"tm": 1 - i}
    to_y = {"groups": 1 - g}
    to_tp = {"tp": 1 - j}

    is_end = lax.rem(lax.div(c + 1, 2), 2) == 0
    e = 1 - lax.rem(lax.div(c + 1, 2), 2)
    is_mid = jnp.logical_not(is_end)
    mate = c + 1 - 2 * lax.rem(c, 2)
    cross = lax.rem(c + 2, N_LINE)
    opp = N_LINE - 1 - c
    first = e * mate + (1 - e) * opp
    second = e * opp + (1 - e) * mate
    slot_first = 2 * (1 - e)
    slot_second = 2 * e
    early = j == i
    late = j != i

    barrier = pltpu.get_barrier_semaphore()
    peers = [to_x, to_y, to_tp, {"ctx": mate}, {"ctx": cross}, {"ctx": opp}, {"tm": 1 - i, "tp": 1 - j}]
    for peer in peers:
        pl.semaphore_signal(barrier, inc=1, device_id=peer, device_id_type=MESH)

    def rows_at(start, size):
        return pl.ds(pl.multiple_of(start, 16), size)

    def cols_at(start, size):
        return pl.ds(pl.multiple_of(start, 128), size)

    own = rows_at(c * rows, rows)
    tok_copy = pltpu.make_async_copy(tokens_hbm, tok_raw.at[c], local_sem.at[6])
    mask_copy = pltpu.make_async_copy(mask_hbm, mask_ref, local_sem.at[9])
    gain_copy = pltpu.make_async_copy(gain_hbm, gain_ref, local_sem.at[7])
    conv_copy = pltpu.make_async_copy(conv_hbm, conv_ref, local_sem.at[8])
    own_depth = rows_at(i * depth, depth)
    in_copies = [
        pltpu.make_async_copy(
            ref.at[:, cols_at(c * hw, hw)],
            w_in.at[own_depth, k * hw : (k + 1) * hw],
            local_sem.at[k],
        )
        for k, ref in enumerate((wq_ref, wk_ref, wv_ref))
    ]
    in_copies.append(
        pltpu.make_async_copy(
            wup_ref.at[:, cols_at(c * fw, fw)],
            w_in.at[own_depth, 3 * hw : 3 * hw + fw],
            local_sem.at[3],
        )
    )
    out_src = wout_ref.at[rows_at(c * hw, hw), :]
    down_src = wdown_ref.at[rows_at(c * fw, fw), :]
    out_rows = rows_at(j * hw, hw)
    down_rows = rows_at(2 * hw + j * fw, fw)
    back_copies = [
        pltpu.make_async_copy(out_src, w_back.at[out_rows], local_sem.at[4]),
        pltpu.make_async_copy(down_src, w_back.at[down_rows], local_sem.at[5]),
    ]
    mask_copy.start()
    tok_copy.start()
    gain_copy.start()
    for copy in in_copies:
        copy.start()
    conv_copy.start()

    @pl.when(early)
    def _():
        for copy in back_copies:
            copy.start()

    sends = []

    def remote(source, target, send, recv, peer):
        return pltpu.make_async_remote_copy(
            src_ref=source,
            dst_ref=target,
            send_sem=send,
            recv_sem=recv,
            device_id=peer,
            device_id_type=MESH,
        )

    def launch(copies, condition=None):
        if condition is None:
            for copy in copies:
                copy.start()
        else:

            @pl.when(condition)
            def _():
                for copy in copies:
                    copy.start()

        sends.append((condition, copies))

    def token_half(block, half):
        return tok_raw.at[block, pl.ds(half * half_frames, half_frames)]

    own_half = tokens_hbm.at[pl.ds(j * half_frames, half_frames)]

    def token_copy(slot, peer, send):
        return remote(own_half, token_half(c, j), tok_send.at[send], tok_recv.at[slot], peer)

    def token_wait(block, slot):
        half = token_half(block, j)
        remote(half, half, tok_send.at[0], tok_recv.at[slot], to_tp).wait_recv()

    pl.semaphore_wait(barrier, len(peers))
    launch(
        [
            token_copy(0, {"ctx": mate}, 1),
            token_copy(2, {"ctx": opp}, 0),
            token_copy(1, {"ctx": cross}, 2),
        ],
        is_end,
    )
    launch([token_copy(2, {"ctx": opp}, 0), token_copy(0, {"ctx": mate}, 1)], is_mid)

    def in_slices(half, owner):
        base = owner * depth + half * part
        out = []
        for k in range(3):
            out.append(w_in.at[rows_at(base, part), k * hw : (k + 1) * hw])
        for k in range(2):
            out.append(w_in.at[rows_at(base + k * (part // 2), part // 2), 3 * hw : 3 * hw + fw])
        return out

    in_sources = [
        ref.at[rows_at(g * part, part), cols_at(c * hw, hw)] for ref in (wq_ref, wk_ref, wv_ref)
    ]
    for k in range(2):
        in_sources.append(
            wup_ref.at[rows_at(g * part + k * (part // 2), part // 2), cols_at(c * fw, fw)]
        )
    x_out = [
        remote(source, ref, x_send.at[k], x_recv.at[k], to_x)
        for k, (source, ref) in enumerate(zip(in_sources, in_slices(g, i)))
    ]
    x_in = [
        remote(ref, ref, x_send.at[k], x_recv.at[k], to_x)
        for k, ref in enumerate(in_slices(g, 1 - i))
    ]
    y_out = [
        remote(ref, ref, y_send.at[k], y_recv.at[k], to_y)
        for k, ref in enumerate(in_slices(g, 1 - i))
    ]
    y_in = [
        remote(ref, ref, y_send.at[k], y_recv.at[k], to_y)
        for k, ref in enumerate(in_slices(1 - g, 1 - i))
    ]
    launch(x_out)

    half_out = hw // 2
    half_down = fw // 2
    quarter_down = fw // 4
    over_peer = {"tm": 1 - i, "tp": i}

    def out_half(core, half):
        return w_back.at[rows_at(core * hw + half * half_out, half_out)]

    def down_late(core):
        return w_back.at[rows_at(2 * hw + core * fw + half_down, half_down)]

    def down_quarter(core, half):
        return w_back.at[rows_at(2 * hw + core * fw + half * quarter_down, quarter_down)]

    launch(
        [
            remote(
                wout_ref.at[rows_at(c * hw + g * half_out, half_out), :],
                out_half(j, g),
                back_send.at[0],
                back_recv.at[j],
                over_peer,
            ),
            remote(
                wdown_ref.at[rows_at(c * fw + g * quarter_down, quarter_down), :],
                down_quarter(j, g),
                back_send.at[2],
                back_recv.at[4 + j],
                over_peer,
            ),
            remote(
                wdown_ref.at[rows_at(c * fw + half_down, half_down), :],
                down_late(j),
                back_send.at[1],
                back_recv.at[2 + j],
                over_peer,
            ),
        ]
    )
    back_in = [
        remote(out_half(core, g), out_half(core, g), back_send.at[0], back_recv.at[core], over_peer)
        for core in range(2)
    ]
    back_in += [
        remote(
            down_quarter(core, g),
            down_quarter(core, g),
            back_send.at[2],
            back_recv.at[4 + core],
            over_peer,
        )
        for core in range(2)
    ]
    down_in = [
        remote(down_late(core), down_late(core), back_send.at[1], back_recv.at[2 + core], over_peer)
        for core in range(2)
    ]
    over_out = [
        remote(out_half(core, g), out_half(core, g), over_send.at[core], over_recv.at[core], to_y)
        for core in range(2)
    ]
    over_in = [
        remote(
            out_half(core, 1 - g), out_half(core, 1 - g), over_send.at[core], over_recv.at[core], to_y
        )
        for core in range(2)
    ]
    over_out += [
        remote(
            down_quarter(core, g),
            down_quarter(core, g),
            over_send.at[2 + core],
            over_recv.at[2 + core],
            to_y,
        )
        for core in range(2)
    ]
    over_in += [
        remote(
            down_quarter(core, 1 - g),
            down_quarter(core, 1 - g),
            over_send.at[2 + core],
            over_recv.at[2 + core],
            to_y,
        )
        for core in range(2)
    ]
    sib_out = [
        remote(out_src, w_back.at[out_rows], sib_send.at[0], sib_recv.at[0], to_tp),
        remote(down_src, w_back.at[down_rows], sib_send.at[1], sib_recv.at[1], to_tp),
    ]
    launch(sib_out, late)
    their_out = w_back.at[rows_at((1 - j) * hw, hw)]
    their_down = w_back.at[rows_at(2 * hw + (1 - j) * fw, fw)]
    sib_in = [
        remote(their_out, their_out, sib_send.at[0], sib_recv.at[0], to_tp),
        remote(their_down, their_down, sib_send.at[1], sib_recv.at[1], to_tp),
    ]
    halo_copy = remote(
        tokens_hbm.at[pl.ds((1 - i) * (frames - 8), 8)],
        halo,
        halo_sem.at[0],
        halo_sem.at[1],
        to_x,
    )
    launch([halo_copy])
    mask_copy.wait()
    row_ids = lax.broadcasted_iota(jnp.int32, (8, 128), 0)
    tile = jnp.zeros((8, 128), jnp.float32)
    for block in range(N_LINE):
        term = (mask_ref[0, block].astype(jnp.float32) - 1.0) * 1e30
        tile = jnp.where(row_ids == block, term, tile)
    bias[c] = tile

    bias_out, bias_in = [], []
    for slot, peer in enumerate((mate, cross, opp)):
        bias_out.append(
            remote(bias.at[c], bias.at[c], bias_send.at[slot], bias_recv.at[slot], {"ctx": peer})
        )
        bias_in.append(
            remote(
                bias.at[peer], bias.at[peer], bias_send.at[slot], bias_recv.at[slot], {"ctx": peer}
            )
        )
    launch(bias_out)

    gain_copy.wait()
    gain = gain_ref[...]

    def norm_block(block):
        at = rows_at(block * rows, rows)
        normed[at, :] = normalised(tok_raw[block].reshape(rows, width), gain)

    def pass_on(index):
        x_in[index].wait_recv()
        launch([y_out[index]])

    def share(block, slot):
        token_wait(block, slot)
        launch(
            [remote(token_half(block, j), token_half(block, j), fwd_send.at[slot], fwd_recv.at[slot], to_tp)]
        )

    def settle(block, slot):
        half = token_half(block, 1 - j)
        remote(half, half, fwd_send.at[slot], fwd_recv.at[slot], to_tp).wait_recv()
        norm_block(block)

    def project(block):
        at = rows_at(block * rows, rows)
        qkv[at, :] = jnp.dot(
            normed[at, :], w_in[:, 0 : 3 * hw], preferred_element_type=jnp.float32
        ).astype(jnp.bfloat16)

    order = [second, cross, first, c]
    att_cols = cols_at(j * hw, hw)
    act_cols = cols_at(2 * hw + j * fw, fw)

    def feature_copy(index, columns, send, recv):
        ref = feats.at[rows_at(order[index] * rows, rows), columns]
        return remote(ref, ref, send.at[index], recv.at[index], to_tp)

    def feed(index):
        at = rows_at(order[index] * rows, rows)
        hidden = jnp.dot(
            normed[at, :], w_in[:, 3 * hw : 3 * hw + fw], preferred_element_type=jnp.float32
        )
        feats[at, act_cols] = jax.nn.gelu(hidden, approximate=True).astype(jnp.bfloat16)
        launch([feature_copy(index, act_cols, act_send, act_recv)])

    def attend(index):
        block = order[index]
        at = rows_at(block * rows, rows)
        marks = bias[block]
        mark = jnp.concatenate([marks[k : k + 1, :] for k in range(N_LINE)], axis=1)
        outs = []
        for head in range(heads):
            low = head * HEAD_DIM
            query = qkv[at, low : low + HEAD_DIM]
            key = qkv[:, hw + low : hw + low + HEAD_DIM]
            value = qkv[:, 2 * hw + low : 2 * hw + low + HEAD_DIM]
            scores = lax.dot_general(
                query, key, (((1,), (1,)), ((), ())), preferred_element_type=jnp.float32
            )
            scores = scores * 0.125 + mark
            peak = jnp.max(scores, axis=-1, keepdims=True)
            expo = jnp.exp(scores - peak)
            total = jnp.sum(expo, axis=-1, keepdims=True)
            mixed = jnp.dot(
                expo.astype(jnp.bfloat16), value, preferred_element_type=jnp.float32
            )
            outs.append(mixed / total)
        feats[at, att_cols] = jnp.concatenate(outs, axis=1).astype(jnp.bfloat16)
        launch([feature_copy(index, att_cols, att_send, att_recv)])

    other_att = cols_at((1 - j) * hw, hw)
    other_act = cols_at(2 * hw + (1 - j) * fw, fw)

    def arrive(slot, send, peer):
        copies = []
        for half in range(PIECES):
            at = slice(half * (rows // PIECES), (half + 1) * (rows // PIECES))
            copies.append(
                remote(
                    summed.at[send, at],
                    arrived.at[slot, at],
                    red_send.at[PIECES * send + half],
                    red_recv.at[PIECES * slot + half],
                    peer,
                )
            )
        return copies

    def wait_arrived(slot, halves):
        copies = arrive(slot, 0, to_tp)
        for half in halves:
            copies[half].wait_recv()

    end_slots = [0, 1, 2]

    def product(index):
        feature_copy(index, other_att, att_send, att_recv).wait_recv()
        feature_copy(index, other_act, act_send, act_recv).wait_recv()
        at = rows_at(order[index] * rows, rows)
        return jnp.dot(feats[at, :], w_back[...], preferred_element_type=jnp.float32)

    def emit(index):
        value = product(index)
        if index == 3:
            mine[2] = value
            return

        @pl.when(is_end)
        def _():
            summed[index] = value.astype(jnp.bfloat16)
            for copy in arrive(end_slots[index], index, {"ctx": mate}):
                copy.start()

        @pl.when(is_mid)
        def _():
            if index == 0:
                summed[0] = value.astype(jnp.bfloat16)
                for copy in arrive(2, 0, {"ctx": mate}):
                    copy.start()
            else:
                mine[index - 1] = value

    def relay(index):
        peer = {"ctx": cross} if index == 1 else {"ctx": opp}
        copies = arrive(3, index, peer)
        for half in range(PIECES):
            at = slice(half * (rows // PIECES), (half + 1) * (rows // PIECES))
            wait_arrived(index - 1, (half,))
            summed[index, at] = (
                mine[index - 1, at] + arrived[index - 1, at].astype(jnp.float32)
            ).astype(jnp.bfloat16)
            copies[half].start()

    def emit_all():
        emit(2)

        @pl.when(is_mid)
        def _():
            relay(1)

        emit(3)

        @pl.when(is_mid)
        def _():
            relay(2)

    tok_copy.wait()
    norm_block(c)
    pass_on(0)
    pass_on(1)
    token_wait(first, slot_first)
    relayed = remote(
        token_half(opp, j), token_half(opp, j), tok_send.at[3], tok_recv.at[1], {"ctx": mate}
    )
    launch([relayed], is_mid)
    launch(
        [
            remote(
                token_half(first, j),
                token_half(first, j),
                fwd_send.at[slot_first],
                fwd_recv.at[slot_first],
                to_tp,
            )
        ]
    )
    pass_on(2)
    settle(first, slot_first)
    pass_on(3)
    share(second, slot_second)
    pass_on(4)
    settle(second, slot_second)
    share(cross, 1)
    for copy in y_in[:3]:
        copy.wait_recv()
    for copy in in_copies:
        copy.wait()
    project(c)
    project(first)
    project(second)
    settle(cross, 1)
    project(cross)

    @pl.when(late)
    def _():
        for core in range(4):
            back_in[core].wait_recv()
            over_out[core].start()

    for copy in bias_in:
        copy.wait_recv()
    attend(0)
    for copy in y_in[3:]:
        copy.wait_recv()
    feed(0)
    attend(1)
    feed(1)

    @pl.when(early)
    def _():
        for copy in back_copies:
            copy.wait()
        for copy in sib_in:
            copy.wait_recv()
        emit(0)

    feed(2)
    feed(3)
    attend(2)

    @pl.when(early)
    def _():
        emit(1)

    @pl.when(late)
    def _():
        for copy in over_in + down_in:
            copy.wait_recv()
        emit(0)
        emit(1)

    attend(3)

    @pl.when(early)
    def _():
        emit(2)

        @pl.when(is_mid)
        def _():
            relay(1)

        emit(3)

        @pl.when(is_mid)
        def _():
            relay(2)

    @pl.when(late)
    def _():
        emit_all()

    conv_copy.wait()
    halo_copy.wait_recv()
    halo_normed[...] = normalised(halo[...].reshape(16, width), gain)
    my_cols = cols_at(j * cols, cols)
    edge = halo_normed[:, my_cols].astype(jnp.float32)
    reach = KERNEL // 2
    extended[0:8, :] = jnp.where(i == 1, edge[8:16], 0.0)
    extended[8 : 8 + rows, :] = normed[own, my_cols].astype(jnp.float32)
    extended[8 + rows : 16 + rows, :] = jnp.where(i == 0, edge[0:8], 0.0)
    base = tok_raw[c, :, :, my_cols].reshape(rows, cols).astype(jnp.float32)
    for tap in range(KERNEL):
        shift = 8 + (tap - reach) * frame
        base = base + conv_ref[tap : tap + 1, :] * extended[shift : shift + rows, :]
    mine[3] = base

    mine[3] = mine[3] + mine[2]
    count = PIECES
    for piece in range(count):
        size = rows // count
        at = slice(piece * size, (piece + 1) * size)
        wait_arrived(2, (piece,))
        part_sum = mine[3, at] + arrived[2, at].astype(jnp.float32)
        wait_arrived(3, (piece,))
        whole = (part_sum + arrived[3, at].astype(jnp.float32)).astype(out_ref.dtype)
        span = frames // count
        out_ref[piece * span : (piece + 1) * span] = whole.reshape(span, dancers, cols)

    @pl.when(late)
    def _():
        for copy in over_out:
            copy.wait_send()

    for index in range(3):
        for copy in arrive(2, index, {"ctx": mate}):
            copy.wait_send()
    for condition, copies in sends:
        if condition is None:
            for copy in copies:
                copy.wait_send()
        else:

            @pl.when(condition)
            def _(copies=copies):
                for copy in copies:
                    copy.wait_send()


def in_one_kernel(
    tokens, norm_gain, block_mask, w_query, w_key, w_value, w_out, w_up, w_down, conv_weight
):
    frames_here, dancers_here, width = tokens.shape
    rows = frames_here * dancers_here
    cols = w_out.shape[1]
    hw = w_query.shape[1] // N_LINE
    fw = w_up.shape[1] // N_LINE
    depth = w_query.shape[0]
    every = N_LINE * rows
    bf16, f32 = jnp.bfloat16, jnp.float32
    vmem = pl.BlockSpec(memory_space=pltpu.VMEM)
    hbm = pl.BlockSpec(memory_space=pltpu.HBM)
    dma = pltpu.SemaphoreType.DMA
    out = pl.pallas_call(
        functools.partial(layer_kernel, dancers_here),
        out_shape=jax.ShapeDtypeStruct((frames_here, dancers_here, cols), bf16),
        in_specs=[hbm] * 10,
        out_specs=vmem,
        scratch_shapes=[
            pltpu.SMEM((1, N_LINE), jnp.int32),
            pltpu.VMEM((1, width), f32),
            pltpu.VMEM(conv_weight.shape, f32),
            pltpu.VMEM((N_LINE,) + tokens.shape, bf16),
            pltpu.VMEM((every, width), bf16),
            pltpu.VMEM((16 // dancers_here, dancers_here, width), bf16),
            pltpu.VMEM((16, width), bf16),
            pltpu.VMEM((N_LINE, 8, 128), f32),
            pltpu.VMEM((2 * depth, 3 * hw + fw), bf16),
            pltpu.VMEM((2 * hw + 2 * fw, cols), bf16),
            pltpu.VMEM((every, 3 * hw), bf16),
            pltpu.VMEM((every, 2 * hw + 2 * fw), bf16),
            pltpu.VMEM((4, rows, cols), f32),
            pltpu.VMEM((3, rows, cols), bf16),
            pltpu.VMEM((4, rows, cols), bf16),
            pltpu.VMEM((rows + 16, cols), f32),
            dma((10,)),
            dma((4,)),
            dma((3,)),
            dma((3,)),
            dma((3,)),
            dma((3,)),
            dma((3,)),
            dma((5,)),
            dma((5,)),
            dma((5,)),
            dma((5,)),
            dma((3,)),
            dma((6,)),
            dma((4,)),
            dma((4,)),
            dma((2,)),
            dma((2,)),
            dma((2,)),
            dma((4,)),
            dma((4,)),
            dma((4,)),
            dma((4,)),
            dma((3 * PIECES,)),
            dma((4 * PIECES,)),
        ],
        compiler_params=pltpu.CompilerParams(
            collective_id=0, has_side_effects=True, vmem_limit_bytes=40 << 20
        ),
    )(
        *[
            pltpu.with_memory_space_constraint(operand, pltpu.HBM)
            for operand in (
                block_mask[0],
                tokens,
                norm_gain[None],
                conv_weight,
                w_query,
                w_key,
                w_value,
                w_up,
                w_out,
                w_down,
            )
        ]
    )
    return out


def solution(mesh):
    def body(tokens, norm_gain, block_mask, w_query, *rest):
        pairs = all(mesh.shape[axis] == 2 for axis in ("groups", "tm", "tp"))
        line = mesh.shape["ctx"] == N_LINE
        rows = tokens.shape[0] * tokens.shape[1]
        split = w_query.shape[1] == 128 * N_LINE and tokens.shape[1] * (KERNEL // 2) <= 8
        if pairs and line and split and rows == 128 and tokens.shape[1] == 2:
            return in_one_kernel(tokens, norm_gain, block_mask, w_query, *rest)
        return on_device(tokens, norm_gain, block_mask, w_query, *rest)

    placed = (
        P(("groups", "tm"), "ctx", None),
        P(),
        P(("groups", "tm"), "ctx", None),
        P("tm", "tp"),
        P("tm", "tp"),
        P("tm", "tp"),
        P("tp", "tm"),
        P("tm", "tp"),
        P("tp", "tm"),
        P(None, "tp"),
    )
    return jax.shard_map(
        body,
        mesh=mesh,
        in_specs=placed,
        out_specs=P(("groups", "tm"), "ctx", "tp"),
        check_vma=False,
    )
```
